128 devices in a mesh: ctx: 32 (over x, y, core), head: 4 (over z).
Axes of the slice: x: 4, y: 4, z: 4, core: 2. Of those that a mesh axis runs over, the one named last changes fastest.
Arguments:
- features_in: bfloat16 [16384, 8192], P('ctx', 'head'), may hold values from -6 to 6
- gate_input: bfloat16 [16384, 8192], P('ctx', 'head'), may hold values from -6 to 6
- state_proj: bfloat16 [16384, 256], P('ctx'), may hold values from -6 to 6
- step_raw: float32 [16384, 128], P('ctx', 'head'), may hold values from -2.1 to 2.1, as said below
- rate_log: float32 [128], P('head'), may hold values from -13 to -2.7, as said below
- conv_features: float32 [4, 8192], P(None, 'head'), may hold values from -3 to 3
- conv_states: float32 [4, 256], replicated, may hold values from -3 to 3
- norm_gain: float32 [8192], P('head'), may hold values from 0.25 to 1.75
- out_weight: bfloat16 [8192, 4096], P('head'), may hold values from -0.09375 to 0.09375
Outputs:
- layer_out: bfloat16 [16384, 4096], P('ctx', 'head')
The draws below stay inside these ranges and needn't reach their ends.
Inputs may be any that keep to these rules, and one draw needn't show every extreme that they name: `rate_log`: per head a decay rate, drawn for each head from one of two ranges: some heads forget within tens of tokens, others keep much of their state over the whole sequence. `step_raw`: varies from token to token and from block to block of tokens.
All inputs are finite; a program needn't handle non-finite values.
Results may differ from the reference program's by a relative error of at most 0.013.
Values may be sent and summed in bfloat16 or wider, within the bound.
A program may use at most 192 MiB of HBM per device.

```python
import jax
import jax.numpy as jnp
from jax import lax

D = 4096
HEADS = 128
HEAD_DIM = 64
STATE = 128
SPAN = 256
INNER = 8192
TOKENS = 16384


def draw_rate_log(key, part):
    pick_key, fast_key, slow_key = jax.random.split(jax.random.fold_in(key, 11), 3)
    fast_share = 0.5
    chosen = jax.random.uniform(pick_key, (HEADS,)) < fast_share
    fast_rate = jnp.log(jax.random.uniform(fast_key, (HEADS,), minval=0.5, maxval=2.0) / 30.0)
    slow_rate = jnp.log(jax.random.uniform(slow_key, (HEADS,), minval=0.3, maxval=1.5) / (0.75 * TOKENS))
    return jnp.where(chosen, fast_rate, slow_rate).astype(jnp.float32)


def draw_step_raw(key, part):
    block_key, noise_key = jax.random.split(jax.random.fold_in(key, 23), 2)
    block_count = (TOKENS + 127) // 128
    levels = jax.random.uniform(block_key, (block_count, HEADS), minval=-1.2, maxval=1.2)
    noise = jnp.clip(0.3 * jax.random.normal(noise_key, (TOKENS, HEADS)), -0.9, 0.9)
    return (jnp.repeat(levels, 128, axis=0)[:TOKENS] + noise).astype(jnp.float32)


def spiked(result, stream_key, source, target, shards_of, factor):
    def block_of(position):
        return (jnp.arange(result.shape[position]) // (result.shape[position] // shards_of)).reshape((-1,) + (1,) * (result.ndim - 1 - position))

    one_side = jax.random.permutation(stream_key, shards_of)[block_of(target)]
    other_side = (block_of(target) + shards_of // 2) % shards_of
    return jnp.where((block_of(source) == one_side) | (block_of(source) == other_side), factor * result, result)


def level_of(rng, dims, pieces, low, largest):
    gain, own = 1.0, jax.random.fold_in(rng, 6)
    for axis_at, parts in pieces:
        steps = jnp.exp(jax.random.uniform(jax.random.fold_in(own, axis_at), (parts,), jnp.float32, low / len(pieces), largest / len(pieces)))
        gain = gain * jnp.repeat(steps, dims[axis_at] // parts).reshape([-1 if axis == axis_at else 1 for axis in range(len(dims))])
    return gain


def bell_draw(key, dims, scale, most, cuts=(), kind=jnp.bfloat16):
    array = scale * jax.random.normal(key, dims, jnp.float32)
    if cuts:
        array = array * level_of(key, dims, cuts, -0.22, 0.18)
    return jnp.clip(array, -most, most).astype(kind)


def gaussian_with(key, dims, deviation, limit, cuts, heavy, kind=jnp.bfloat16):
    entries = deviation * jax.random.normal(key, dims, jnp.float32)
    if cuts:
        entries = entries * level_of(key, dims, cuts, -0.22, 0.18)
    return jnp.clip(spiked(entries, jax.random.fold_in(key, 3), *heavy), -limit, limit).astype(kind)


def setup_inputs(seed: int = 0) -> dict:
    seeds = jax.random.split(jax.random.key(seed), 10)
    return {
        "features_in": bell_draw(seeds[0], (TOKENS, INNER), 1.0, 6.0, ((0, 32), (1, 4))),
        "gate_input": bell_draw(seeds[1], (TOKENS, INNER), 1.0, 6.0, ((0, 32), (1, 4))),
        "state_proj": bell_draw(seeds[2], (TOKENS, 2 * STATE), 1.0, 6.0, ((0, 32),)),
        "step_raw": draw_step_raw(jax.random.fold_in(seeds[9], 71), 0),
        "rate_log": draw_rate_log(jax.random.fold_in(seeds[9], 71), 0),
        "conv_features": bell_draw(seeds[5], (4, INNER), 4 ** -0.5, 3.0, ((1, 4),), jnp.float32),
        "conv_states": bell_draw(seeds[6], (4, 2 * STATE), 4 ** -0.5, 3.0, (), jnp.float32),
        "norm_gain": jnp.clip(1.0 + 0.15 * jax.random.normal(seeds[7], (INNER,), jnp.float32), 0.25, 1.75),
        "out_weight": gaussian_with(seeds[8], (INNER, D), INNER ** -0.5, 0.09375, ((0, 4),), (0, 1, 4, 2.0)),
    }


def causal_conv(series, kernel):
    length = series.shape[0]
    padded = jnp.pad(series.astype(jnp.float32), ((3, 0), (0, 0)))
    summed = padded[0:length] * kernel[0]
    for offset in range(1, 4):
        summed = summed + padded[offset:offset + length] * kernel[offset]
    return jax.nn.silu(summed).astype(jnp.bfloat16)

def reference(features_in, gate_input, state_proj, step_raw, rate_log, conv_features, conv_states, norm_gain, out_weight):
    features = causal_conv(features_in, conv_features)
    states_conv = causal_conv(state_proj, conv_states)
    key_side = states_conv[:, :STATE]
    query_side = states_conv[:, STATE:]
    step_size = jax.nn.softplus(step_raw)
    log_decay = -step_size * jnp.exp(rate_log)[None, :]
    inputs = (features.astype(jnp.float32).reshape(TOKENS, HEADS, HEAD_DIM) * step_size[:, :, None]).astype(jnp.bfloat16)
    blocks = TOKENS // SPAN
    causal = jnp.tril(jnp.ones((SPAN, SPAN), dtype=bool))[:, :, None]

    def advance(running, element):
        decay_part, key_part, query_part, input_part = element
        cum_decay = jnp.cumsum(decay_part, axis=0)
        scores = jnp.dot(query_part, key_part.T, preferred_element_type=jnp.float32)
        spread = cum_decay[:, None, :] - cum_decay[None, :, :]
        decays = jnp.where(causal, jnp.exp(jnp.where(causal, spread, 0.0)), 0.0)
        weights = (scores[:, :, None] * decays).astype(jnp.bfloat16)
        intra_out = jnp.einsum('ijh,jhp->ihp', weights.astype(jnp.float32), input_part.astype(jnp.float32))
        from_state = jnp.einsum('in,hpn->ihp', query_part.astype(jnp.float32), running, precision=lax.Precision.HIGHEST)
        outputs = intra_out + jnp.exp(cum_decay)[:, :, None] * from_state
        span_total = cum_decay[-1]
        scaled_key = (jnp.exp(span_total[None, :] - cum_decay)[:, :, None] * key_part.astype(jnp.float32)[:, None, :]).astype(jnp.bfloat16)
        contrib = jnp.einsum('jhn,jhp->hpn', scaled_key.astype(jnp.float32), input_part.astype(jnp.float32))
        return (jnp.exp(span_total)[:, None, None] * running + contrib, outputs)
    initial = jnp.zeros((HEADS, HEAD_DIM, STATE), jnp.float32)
    carried = (log_decay.reshape(blocks, SPAN, HEADS), key_side.reshape(blocks, SPAN, STATE), query_side.reshape(blocks, SPAN, STATE), inputs.reshape(blocks, SPAN, HEADS, HEAD_DIM))
    final_state, ssd = lax.scan(advance, initial, carried)
    ssd = ssd.reshape(TOKENS, HEADS, HEAD_DIM)
    gated = ssd * jax.nn.silu(gate_input.astype(jnp.float32)).reshape(TOKENS, HEADS, HEAD_DIM)
    mean_square = lax.optimization_barrier(jnp.mean(gated * gated, axis=-1, keepdims=True))
    normed = (gated * lax.rsqrt(mean_square + 1e-05) * norm_gain.reshape(HEADS, HEAD_DIM)).reshape(TOKENS, INNER).astype(jnp.bfloat16)
    return jnp.dot(normed, out_weight, preferred_element_type=jnp.float32).astype(jnp.bfloat16)
```

```python
import functools

import jax
import jax.numpy as jnp
from jax import lax
from jax.experimental import pallas as pl
from jax.experimental.pallas import tpu as pltpu
from jax.sharding import PartitionSpec as P

HEAD_DIM = 64
STATE = 128
MESH = pl.DeviceIdType.MESH
F32 = jnp.float32
BF16 = jnp.bfloat16

LEAD = 16
ROWS = 64
BLOCK = 128
COLS = 256
SLAB = 64


def dot(a, b):
    return jnp.dot(a, b, preferred_element_type=F32)


def silu(x):
    half = 0.5 * x
    return half + half * jnp.tanh(half)


def iota(shape, axis):
    return lax.broadcasted_iota(jnp.int32, shape, axis)


def in_three(value, group):
    high = value.astype(BF16).astype(F32)
    rest = value - high
    mid = rest.astype(BF16).astype(F32)
    low = rest - mid
    none = jnp.zeros_like(value)
    parts = jnp.where(group == 0, high, jnp.where(group == 1, mid, jnp.where(group == 2, low, none)))
    return parts.astype(BF16)


def layer(
    nctx,
    nhead,
    feat_h,
    gate_h,
    st_h,
    step_h,
    rate_h,
    taps_h,
    staps_h,
    gain_h,
    w_h,
    out_h,
    featb,
    gateb,
    stb,
    bordf,
    bords,
    stepb,
    rateb,
    tapsb,
    stapsb,
    gainb,
    wb,
    ab,
    yb,
    xb,
    db,
    kb,
    qb,
    kt,
    mb,
    a3,
    e3,
    oh,
    oht,
    rowsb,
    tot,
    fade,
    slab_s,
    slab_r,
    ret_s,
    inc,
    rel_s,
    rel_r,
    p_s,
    p_r,
    r_s,
    r_r,
    own,
    lsem,
    bsem,
    ts,
    tr,
    fs,
    fr,
    gs,
    gr,
    js,
    jr,
):
    tokens, feats = gate_h.shape
    half_t = tokens // 2
    outs = out_h.shape[1]
    half_o = outs // 2
    ncb = feats // COLS
    nrow = tokens // ROWS
    nblk = tokens // BLOCK
    me = lax.axis_index("ctx")
    z = lax.axis_index("head")

    loads = [
        (step_h, stepb),
        (rate_h, rateb),
        (taps_h, tapsb),
        (feat_h, featb.at[pl.ds(LEAD, tokens), :]),
        (st_h, stb.at[pl.ds(LEAD, tokens), :]),
        (staps_h, stapsb),
        (gate_h, gateb),
        (gain_h, gainb),
        (w_h, wb),
    ]
    loads = [pltpu.make_async_copy(s, d, lsem.at[i]) for i, (s, d) in enumerate(loads)]
    for load in loads[:6]:
        load.start()

    barrier = pltpu.get_barrier_semaphore()

    def greet(k, _):
        pl.semaphore_signal(
            barrier, inc=1, device_id={"ctx": lax.rem(me + k, nctx)}, device_id_type=MESH
        )
        return 0

    lax.fori_loop(1, nctx, greet, 0)
    for k in (1, nhead - 1):
        pl.semaphore_signal(
            barrier, inc=1, device_id={"head": lax.rem(z + k, nhead)}, device_id_type=MESH
        )

    group = iota((tokens, 128), 1) // 32
    loads[0].wait()
    loads[1].wait()
    raw = jnp.concatenate([stepb[...]] * 4, axis=0).T
    step = jnp.maximum(raw, 0.0) + jnp.log(1.0 + jnp.exp(-jnp.abs(raw)))
    rate = jnp.concatenate([rateb[...]] * 4, axis=1)
    decay = in_three(-step * jnp.exp(rate), group)
    tri = jnp.where(iota((tokens, tokens), 0) >= iota((tokens, tokens), 1), 1.0, 0.0).astype(BF16)
    thirds = dot(tri, decay)
    cum = (
        thirds
        + pltpu.roll(thirds, 32, 1)
        + pltpu.roll(thirds, 64, 1)
        + pltpu.roll(thirds, 96, 1)
    )
    tot[me] = cum[tokens - 1 : tokens]
    centre = cum[half_t - 1 : half_t]
    total = cum[tokens - 1 : tokens]
    away = cum - centre
    a3[...] = in_three(step * jnp.exp(-away), group)
    e3[...] = in_three(jnp.exp(away), group)
    oh[...] = jnp.where((iota((128, feats), 0) & 31) == iota((128, feats), 1) // HEAD_DIM, 1.0, 0.0).astype(BF16)
    oht[...] = jnp.where(
        (iota((feats, 128), 1) & 31) == iota((feats, 128), 0) // HEAD_DIM, 1.0 / HEAD_DIM, 0.0
    ).astype(BF16)
    line = iota((16, 128), 0)
    scales = jnp.where(line == 0, jnp.exp(total - centre), jnp.exp(centre))
    rowsb[...] = dot(in_three(scales, iota((16, 128), 1) // 32), oh[...])

    def conv(x, taps):
        total = x * taps[3:4]
        for back in range(1, 4):
            total = total + pltpu.roll(x, back, 0) * taps[3 - back : 4 - back]
        return silu(total[LEAD:])

    def columns(cb):
        return pl.ds(pl.multiple_of(cb * COLS, COLS), COLS)

    featb[0:LEAD, :] = jnp.zeros((LEAD, feats), BF16)
    stb[0:LEAD, :] = jnp.zeros((LEAD, 2 * STATE), BF16)
    loads[2].wait()
    loads[3].wait()
    for load in loads[6:]:
        load.start()

    def feature_block(cb, _):
        cols = columns(cb)
        ab[:, cols] = dot(a3[...], oh[:, cols])

        def chunk(r, _):
            at = pl.multiple_of(r * ROWS, ROWS)
            x = featb[pl.ds(at, ROWS + LEAD), cols].astype(F32)
            v = conv(x, tapsb[:, cols]) * ab[pl.ds(at, ROWS), cols]
            xb[pl.ds(at, ROWS), cols] = v.astype(BF16)
            return 0

        return lax.fori_loop(0, nrow, chunk, 0, unroll=True)

    lax.fori_loop(0, ncb, feature_block, 0)
    loads[4].wait()
    loads[5].wait()

    def states(r, _):
        at = pl.multiple_of(r * ROWS, ROWS)
        v = conv(stb[pl.ds(at, ROWS + LEAD), :].astype(F32), stapsb[...])
        kb[pl.ds(at, ROWS), :] = v[:, :STATE].astype(BF16).astype(F32)
        qb[pl.ds(at, ROWS), :] = v[:, STATE:].astype(BF16)
        return 0

    lax.fori_loop(0, nrow, states, 0, unroll=True)
    later = iota((tokens, STATE), 0) >= LEAD
    kt[...] = jnp.where(later, kb[...], 0.0).T.astype(BF16)

    def state_block(cb, _):
        cols = columns(cb)
        db[:, cols] = dot(kt[...], xb[:, cols])
        return 0

    lax.fori_loop(0, ncb, state_block, 0, unroll=2)

    pl.semaphore_wait(barrier, nctx + 1)
    after = lax.rem(me + 1, nctx)
    borders = [
        pltpu.make_async_remote_copy(
            src_ref=src.at[pl.ds(tokens, LEAD), :],
            dst_ref=dst,
            send_sem=bsem.at[i],
            recv_sem=bsem.at[2 + i],
            device_id={"ctx": after},
            device_id_type=MESH,
        )
        for i, (src, dst) in enumerate(((featb, bordf), (stb, bords)))
    ]

    @pl.when(me < nctx - 1)
    def _():
        for border in borders:
            border.start()

    @pl.when(me == 0)
    def _():
        bordf[...] = jnp.zeros((LEAD, feats), BF16)
        bords[...] = jnp.zeros((LEAD, 2 * STATE), BF16)

    def total_copy(slot, to):
        return pltpu.make_async_remote_copy(
            src_ref=tot.at[slot],
            dst_ref=tot.at[slot],
            send_sem=ts.at[to],
            recv_sem=tr.at[slot],
            device_id={"ctx": to},
            device_id_type=MESH,
        )

    def send_total(k, _):
        total_copy(me, lax.rem(me + k, nctx)).start()
        return 0

    lax.fori_loop(1, nctx, send_total, 0)

    @pl.when(me > 0)
    def _():
        for border in borders:
            border.wait_recv()

    v = conv(jnp.concatenate([bords[...], stb[LEAD : 2 * LEAD, :]], axis=0).astype(F32), stapsb[...])
    kb[0:LEAD, :] = v[:, :STATE].astype(BF16).astype(F32)
    qb[0:LEAD, :] = v[:, STATE:].astype(BF16)
    for cb in range(ncb):
        cols = slice(cb * COLS, (cb + 1) * COLS)
        x = jnp.concatenate([bordf[:, cols], featb[LEAD : 2 * LEAD, cols]], axis=0).astype(F32)
        xb[0:LEAD, cols] = (conv(x, tapsb[:, cols]) * ab[0:LEAD, cols]).astype(BF16)

    first = jnp.where(iota((128, STATE), 0) < LEAD, kb[0:128, :], 0.0).T.astype(BF16)

    def slab_copy(src, slot, to):
        return pltpu.make_async_remote_copy(
            src_ref=slab_s.at[src],
            dst_ref=slab_r.at[slot],
            send_sem=fs.at[src],
            recv_sem=fr.at[slot],
            device_id={"ctx": to},
            device_id_type=MESH,
        )

    for part in range(2):
        rows = slice(part * SLAB, (part + 1) * SLAB)
        for cb in range(ncb):
            cols = slice(cb * COLS, (cb + 1) * COLS)
            d = db[rows, cols] + dot(first[rows], xb[0:128, cols])
            d = (d * rowsb[0:1, cols]).astype(BF16)
            for pair in range(COLS // 128):
                slab_s[(cb * (COLS // 128) + pair) * 2 + part] = d[:, pair * 128 : pair * 128 + 128]

        def send_slab(k, _):
            to = 2 * lax.rem(me // 2 + k, nctx // 2) + part

            @pl.when(to != me)
            def _():
                slab_copy(to, me, to).start()

            return 0

        lax.fori_loop(0, nctx // 2, send_slab, 0)
    slab_r[me] = slab_s[me]
    kt[...] = kb[...].T.astype(BF16)

    for i in range(2):
        score = dot(qb[i * half_t : (i + 1) * half_t, :], kt[...])
        keep = iota((half_t, tokens), 0) + i * half_t >= iota((half_t, tokens), 1)
        mb[i * half_t : (i + 1) * half_t, :] = jnp.where(keep, score, 0.0).astype(BF16)

    def intra(cb, _):
        cols = columns(cb)
        yb[0:half_t, cols] = dot(mb[0:half_t, 0:half_t], xb[0:half_t, cols])
        yb[half_t:tokens, cols] = dot(mb[half_t:tokens, :], xb[:, cols])
        return 0

    lax.fori_loop(0, ncb, intra, 0)

    def back_copy(src, owner, to):
        rows = pl.ds(pl.multiple_of(lax.rem(owner, 2) * SLAB, SLAB), SLAB)
        lanes = pl.ds(pl.multiple_of((owner // 2) * 128, 128), 128)
        return pltpu.make_async_remote_copy(
            src_ref=ret_s.at[src],
            dst_ref=inc.at[rows, lanes],
            send_sem=gs.at[src],
            recv_sem=gr.at[owner],
            device_id={"ctx": to},
            device_id_type=MESH,
        )

    def total_here(e, _):
        @pl.when(e != me)
        def _():
            total_copy(e, e).wait_recv()

        return 0

    lax.fori_loop(0, nctx, total_here, 0)
    lanes = pl.ds(pl.multiple_of((me // 2) * 128, 128), 128)
    everyone = in_three(tot[...].reshape(nctx, 128), iota((nctx, 128), 1) // 32)
    fade[...] = jnp.exp(dot(everyone, oh[:, lanes])).reshape(nctx, 1, 128)

    def slab_here(e, _):
        @pl.when(e != me)
        def _():
            slab_copy(e, e, e).wait_recv()

        return 0

    lax.fori_loop(0, nctx, slab_here, 0)

    def scan(i, run):
        for e in range(8):
            ret_s[i * 8 + e] = run.astype(BF16)
            run = fade[i * 8 + e] * run + slab_r[i * 8 + e].astype(F32)
        return run

    lax.fori_loop(0, nctx // 8, scan, jnp.zeros((SLAB, 128), F32))

    def send_back(k, _):
        to = lax.rem(me + k, nctx)
        back_copy(to, me, to).start()
        return 0

    lax.fori_loop(1, nctx, send_back, 0)
    inc[
        pl.ds(pl.multiple_of(lax.rem(me, 2) * SLAB, SLAB), SLAB),
        pl.ds(pl.multiple_of((me // 2) * 128, 128), 128),
    ] = ret_s[me]

    loads[6].wait()

    def gate_block(i, _):
        cols = columns(i // 4)
        at = pl.ds(pl.multiple_of(lax.rem(i, 4) * 128, 128), 128)
        ab[at, cols] = dot(e3[at, :], oh[:, cols]) * silu(gateb[at, cols].astype(F32))
        return 0

    lax.fori_loop(0, ncb * 4, gate_block, 0)
    loads[7].wait()
    loads[8].wait()

    def arrived(e, _):
        @pl.when(e != me)
        def _():
            back_copy(e, e, e).wait_recv()

        return 0

    lax.fori_loop(0, nctx, arrived, 0)

    group_n = iota((BLOCK, 128), 1) // 32

    def block_rows(b):
        return pl.ds(pl.multiple_of(b * BLOCK, BLOCK), BLOCK)

    def norm_block(b):
        at = block_rows(b)
        mean = jnp.zeros((BLOCK, 128), F32)
        for cb in range(ncb):
            cols = slice(cb * COLS, (cb + 1) * COLS)
            y = dot(qb[at, :], inc[:, cols]) * rowsb[1:2, cols] + yb[at, cols]
            y = y * ab[at, cols]
            yb[at, cols] = y
            mean = mean + dot((y * y).astype(BF16), oht[cols, :])
        scale = in_three(lax.rsqrt(mean + 1e-05), group_n)
        for cb in range(ncb):
            cols = slice(cb * COLS, (cb + 1) * COLS)
            xb[at, cols] = (yb[at, cols] * dot(scale, oh[:, cols]) * gainb[:, cols]).astype(BF16)

    def project(b, dest, half):
        cols = pl.ds(pl.multiple_of(dest * outs + half * half_o, half_o), half_o)
        return dot(xb[block_rows(b), :], wb[:, cols])

    def towards(side):
        return lax.rem(z + 1 + side * (nhead - 2), nhead)

    def job_copy(src, dst, side, b, first):
        i = (first * nblk + b) * 2 + side
        return pltpu.make_async_remote_copy(
            src_ref=src.at[side, b],
            dst_ref=dst.at[side, b],
            send_sem=js.at[i],
            recv_sem=jr.at[i],
            device_id={"head": towards(side)},
            device_id_type=MESH,
        )

    def relay_block(b, _):
        norm_block(b)

        def one(side, _):
            rel_s[side, b] = project(b, lax.rem(z + 2, nhead), side).astype(BF16)
            job_copy(rel_s, rel_r, side, b, 0).start()
            return 0

        return lax.fori_loop(0, 2, one, 0)

    lax.fori_loop(0, nblk, relay_block, 0)

    def plain(i, _):
        b, side = i // 2, lax.rem(i, 2)
        p_s[side, b] = project(b, towards(side), 1 - side).astype(BF16)
        job_copy(p_s, p_r, side, b, 1).start()
        return 0

    lax.fori_loop(0, 2 * nblk, plain, 0)

    def relayed(i, _):
        b, side = i // 2, lax.rem(i, 2)
        part = project(b, towards(side), side)
        job_copy(rel_s, rel_r, side, b, 0).wait_recv()
        r_s[side, b] = (part + rel_r[side, b].astype(F32)).astype(BF16)
        job_copy(r_s, r_r, side, b, 2).start()
        return 0

    lax.fori_loop(0, 2 * nblk, relayed, 0)

    def mine(i, _):
        b, half = i // 2, lax.rem(i, 2)
        own[half, b] = project(b, z, half)
        return 0

    lax.fori_loop(0, 2 * nblk, mine, 0)

    @pl.when(me < nctx - 1)
    def _():
        for border in borders:
            border.wait_send()

    def left(k, _):
        to = lax.rem(me + k, nctx)
        slab_copy(to, me, to).wait_send()
        back_copy(to, me, to).wait_send()
        total_copy(me, to).wait_send()
        return 0

    lax.fori_loop(1, nctx, left, 0)

    def jobs_left(i, _):
        b, side = i // 2, lax.rem(i, 2)
        job_copy(rel_s, rel_r, side, b, 0).wait_send()
        job_copy(p_s, p_r, side, b, 1).wait_send()
        return 0

    lax.fori_loop(0, 2 * nblk, jobs_left, 0)

    def finish(i, _):
        b, half = i // 2, lax.rem(i, 2)
        job_copy(p_s, p_r, 1 - half, b, 1).wait_recv()
        job_copy(r_s, r_r, half, b, 2).wait_send()
        job_copy(r_s, r_r, half, b, 2).wait_recv()
        total = own[half, b] + p_r[1 - half, b].astype(F32) + r_r[half, b].astype(F32)
        out_h[block_rows(b), pl.ds(pl.multiple_of(half * half_o, half_o), half_o)] = total.astype(BF16)
        return 0

    lax.fori_loop(0, 2 * nblk, finish, 0)


def per_device(
    nctx,
    nhead,
    features_in,
    gate_input,
    state_proj,
    step_raw,
    rate_log,
    conv_features,
    conv_states,
    norm_gain,
    out_weight,
):
    tokens, feats = features_in.shape
    heads = rate_log.shape[0]
    outs = out_weight.shape[1] // nhead
    half_o = outs // 2
    any_space = pl.BlockSpec(memory_space=pltpu.HBM)
    vmem = pltpu.VMEM
    dma = pltpu.SemaphoreType.DMA
    job = (2, tokens // BLOCK, BLOCK, half_o)
    scratch = [
        vmem((LEAD + tokens, feats), BF16),
        vmem((tokens, feats), BF16),
        vmem((LEAD + tokens, 2 * STATE), BF16),
        vmem((LEAD, feats), BF16),
        vmem((LEAD, 2 * STATE), BF16),
        vmem((heads, tokens), F32),
        vmem((1, heads), F32),
        vmem((4, feats), F32),
        vmem((4, 2 * STATE), F32),
        vmem((1, feats), F32),
        vmem(out_weight.shape, BF16),
        vmem((tokens, feats), F32),
        vmem((tokens, feats), F32),
        vmem((tokens, feats), BF16),
        vmem((STATE, feats), F32),
        vmem((tokens, STATE), F32),
        vmem((tokens, STATE), BF16),
        vmem((STATE, tokens), BF16),
        vmem((tokens, tokens), BF16),
        vmem((tokens, 128), BF16),
        vmem((tokens, 128), BF16),
        vmem((128, feats), BF16),
        vmem((feats, 128), BF16),
        vmem((16, feats), F32),
        vmem((nctx, 1, 128), F32),
        vmem((nctx, 1, 128), F32),
        vmem((nctx, SLAB, 128), BF16),
        vmem((nctx, SLAB, 128), BF16),
        vmem((nctx, SLAB, 128), BF16),
        vmem((STATE, feats), BF16),
        vmem(job, BF16),
        vmem(job, BF16),
        vmem(job, BF16),
        vmem(job, BF16),
        vmem(job, BF16),
        vmem(job, BF16),
        vmem(job, F32),
        dma((9,)),
        dma((4,)),
        dma((nctx,)),
        dma((nctx,)),
        dma((nctx,)),
        dma((nctx,)),
        dma((nctx,)),
        dma((nctx,)),
        dma((6 * (tokens // BLOCK),)),
        dma((6 * (tokens // BLOCK),)),
    ]
    return pl.pallas_call(
        functools.partial(layer, nctx, nhead),
        out_shape=jax.ShapeDtypeStruct((tokens, outs), BF16),
        in_specs=[any_space] * 9,
        out_specs=pl.BlockSpec(memory_space=pltpu.VMEM),
        scratch_shapes=scratch,
        compiler_params=pltpu.CompilerParams(collective_id=0, has_side_effects=True, vmem_limit_bytes=52 * 1024 * 1024),
        name="ssd_layer",
    )(
        *(
            pltpu.with_memory_space_constraint(a, pltpu.HBM)
            for a in (
                features_in,
                gate_input,
                state_proj,
                step_raw.T,
                rate_log.reshape(1, heads),
                conv_features,
                conv_states,
                norm_gain.reshape(1, feats),
                out_weight,
            )
        )
    )


def solution(mesh):
    placed = (
        P("ctx", "head"),
        P("ctx", "head"),
        P("ctx", None),
        P("ctx", "head"),
        P("head"),
        P(None, "head"),
        P(),
        P("head"),
        P("head", None),
    )
    body = functools.partial(per_device, mesh.shape["ctx"], mesh.shape["head"])
    return jax.shard_map(
        body, mesh=mesh, in_specs=placed, out_specs=P("ctx", "head"), check_vma=False
    )
```

```python
import functools

import jax
import jax.numpy as jnp
from jax import lax
from jax.experimental import pallas as pl
from jax.experimental.pallas import tpu as pltpu
from jax.sharding import PartitionSpec as P

HEAD_DIM = 64
STATE = 128
MESH = pl.DeviceIdType.MESH
F32 = jnp.float32
BF16 = jnp.bfloat16

LEAD = 16
ROWS = 64
BLOCK = 128
COLS = 256
SLAB = 64


def dot(a, b):
    return jnp.dot(a, b, preferred_element_type=F32)


def silu(x):
    half = 0.5 * x
    return half + half * jnp.tanh(half)


def iota(shape, axis):
    return lax.broadcasted_iota(jnp.int32, shape, axis)


def in_three(value, group):
    high = value.astype(BF16).astype(F32)
    rest = value - high
    mid = rest.astype(BF16).astype(F32)
    low = rest - mid
    none = jnp.zeros_like(value)
    parts = jnp.where(group == 0, high, jnp.where(group == 1, mid, jnp.where(group == 2, low, none)))
    return parts.astype(BF16)


def layer(
    nctx,
    nhead,
    feat_h,
    gate_h,
    st_h,
    step_h,
    rate_h,
    taps_h,
    staps_h,
    gain_h,
    w_h,
    out_h,
    featb,
    gateb,
    stb,
    bordf,
    bords,
    stepb,
    rateb,
    tapsb,
    stapsb,
    gainb,
    wb,
    ab,
    yb,
    xb,
    db,
    kb,
    qb,
    kt,
    mb,
    a3,
    e3,
    oh,
    oht,
    rowsb,
    tot,
    fade,
    slab_s,
    slab_r,
    ret_s,
    inc,
    rel_s,
    rel_r,
    p_s,
    p_r,
    r_s,
    r_r,
    own,
    lsem,
    bsem,
    csem,
    js,
    jr,
):
    tokens, feats = gate_h.shape
    half_t = tokens // 2
    outs = out_h.shape[1]
    half_o = outs // 2
    ncb = feats // COLS
    nrow = tokens // ROWS
    nblk = tokens // BLOCK
    me = lax.axis_index("ctx")
    z = lax.axis_index("head")

    loads = [
        (step_h, stepb),
        (rate_h, rateb),
        (st_h, stb.at[pl.ds(LEAD, tokens), :]),
        (staps_h, stapsb),
        (taps_h, tapsb),
        (feat_h, featb.at[pl.ds(LEAD, tokens), :]),
        (gate_h, gateb),
        (gain_h, gainb),
        (w_h, wb),
    ]
    loads = [pltpu.make_async_copy(s, d, lsem.at[i]) for i, (s, d) in enumerate(loads)]
    for load in loads[:6]:
        load.start()

    barrier = pltpu.get_barrier_semaphore()

    def greet(k, _):
        pl.semaphore_signal(
            barrier, inc=1, device_id={"ctx": lax.rem(me + k, nctx)}, device_id_type=MESH
        )
        return 0

    lax.fori_loop(1, nctx, greet, 0)
    for k in (1, nhead - 1):
        pl.semaphore_signal(
            barrier, inc=1, device_id={"head": lax.rem(z + k, nhead)}, device_id_type=MESH
        )

    group = iota((tokens, 128), 1) // 32
    tri = jnp.where(iota((tokens, tokens), 0) >= iota((tokens, tokens), 1), 1.0, 0.0).astype(BF16)
    oh[...] = jnp.where((iota((128, feats), 0) & 31) == iota((128, feats), 1) // HEAD_DIM, 1.0, 0.0).astype(BF16)
    oht[...] = jnp.where(
        (iota((feats, 128), 1) & 31) == iota((feats, 128), 0) // HEAD_DIM, 1.0 / HEAD_DIM, 0.0
    ).astype(BF16)
    featb[0:LEAD, :] = jnp.zeros((LEAD, feats), BF16)
    stb[0:LEAD, :] = jnp.zeros((LEAD, 2 * STATE), BF16)
    loads[0].wait()
    loads[1].wait()
    raw = jnp.concatenate([stepb[...]] * 4, axis=0).T
    step = jnp.maximum(raw, 0.0) + jnp.log(1.0 + jnp.exp(-jnp.abs(raw)))
    rate = jnp.concatenate([rateb[...]] * 4, axis=1)
    decay = in_three(-step * jnp.exp(rate), group)
    thirds = dot(tri, decay)
    cum = (
        thirds
        + pltpu.roll(thirds, 32, 1)
        + pltpu.roll(thirds, 64, 1)
        + pltpu.roll(thirds, 96, 1)
    )
    tot[me] = cum[tokens - 1 : tokens]
    centre = cum[half_t - 1 : half_t]
    total = cum[tokens - 1 : tokens]
    away = cum - centre
    a3[...] = in_three(step * jnp.exp(-away), group)
    e3[...] = in_three(jnp.exp(away), group)
    line = iota((16, 128), 0)
    scales = jnp.where(line == 0, jnp.exp(total - centre), jnp.exp(centre))
    rowsb[...] = dot(in_three(scales, iota((16, 128), 1) // 32), oh[...])

    def conv(x, taps):
        total = x * taps[3:4]
        for back in range(1, 4):
            total = total + pltpu.roll(x, back, 0) * taps[3 - back : 4 - back]
        return silu(total[LEAD:])

    def columns(cb):
        return pl.ds(pl.multiple_of(cb * COLS, COLS), COLS)

    loads[2].wait()
    loads[3].wait()

    def states(r, _):
        at = pl.multiple_of(r * ROWS, ROWS)
        v = conv(stb[pl.ds(at, ROWS + LEAD), :].astype(F32), stapsb[...])
        kb[pl.ds(at, ROWS), :] = v[:, :STATE].astype(BF16).astype(F32)
        qb[pl.ds(at, ROWS), :] = v[:, STATE:].astype(BF16)
        return 0

    lax.fori_loop(0, nrow, states, 0, unroll=True)
    later = iota((tokens, STATE), 0) >= LEAD
    kt[...] = jnp.where(later, kb[...], 0.0).T.astype(BF16)

    loads[4].wait()
    loads[5].wait()
    for load in loads[6:]:
        load.start()

    def feature_block(cb):
        cols = columns(cb)
        ab[:, cols] = dot(a3[...], oh[:, cols])

        def chunk(r, _):
            at = pl.multiple_of(r * ROWS, ROWS)
            x = featb[pl.ds(at, ROWS + LEAD), cols].astype(F32)
            v = conv(x, tapsb[:, cols]) * ab[pl.ds(at, ROWS), cols]
            xb[pl.ds(at, ROWS), cols] = v.astype(BF16)
            return 0

        lax.fori_loop(0, nrow, chunk, 0, unroll=True)

    def state_block(cb):
        cols = columns(cb)
        db[:, cols] = dot(kt[...], xb[:, cols])

    def both(cb, _):
        state_block(cb - 1)
        feature_block(cb)
        return 0

    feature_block(0)
    lax.fori_loop(1, ncb // 2, both, 0)

    pl.semaphore_wait(barrier, nctx + 1)
    after = lax.rem(me + 1, nctx)
    borders = [
        pltpu.make_async_remote_copy(
            src_ref=src.at[pl.ds(tokens, LEAD), :],
            dst_ref=dst,
            send_sem=bsem.at[i],
            recv_sem=bsem.at[2 + i],
            device_id={"ctx": after},
            device_id_type=MESH,
        )
        for i, (src, dst) in enumerate(((featb, bordf), (stb, bords)))
    ]

    @pl.when(me < nctx - 1)
    def _():
        for border in borders:
            border.start()

    @pl.when(me == 0)
    def _():
        bordf[...] = jnp.zeros((LEAD, feats), BF16)
        bords[...] = jnp.zeros((LEAD, 2 * STATE), BF16)

    lax.fori_loop(ncb // 2, ncb, both, 0)
    state_block(ncb - 1)

    @pl.when(me > 0)
    def _():
        for border in borders:
            border.wait_recv()

    v = conv(jnp.concatenate([bords[...], stb[LEAD : 2 * LEAD, :]], axis=0).astype(F32), stapsb[...])
    kb[0:LEAD, :] = v[:, :STATE].astype(BF16).astype(F32)
    qb[0:LEAD, :] = v[:, STATE:].astype(BF16)
    for cb in range(ncb):
        cols = slice(cb * COLS, (cb + 1) * COLS)
        x = jnp.concatenate([bordf[:, cols], featb[LEAD : 2 * LEAD, cols]], axis=0).astype(F32)
        xb[0:LEAD, cols] = (conv(x, tapsb[:, cols]) * ab[0:LEAD, cols]).astype(BF16)

    first = jnp.where(iota((128, STATE), 0) < LEAD, kb[0:128, :], 0.0).T.astype(BF16)

    def total_copy(to):
        return pltpu.make_async_remote_copy(
            src_ref=tot.at[me],
            dst_ref=tot.at[me],
            send_sem=csem.at[0],
            recv_sem=csem.at[1],
            device_id={"ctx": to},
            device_id_type=MESH,
        )

    def slab_copy(to):
        return pltpu.make_async_remote_copy(
            src_ref=slab_s.at[to],
            dst_ref=slab_r.at[me],
            send_sem=csem.at[2],
            recv_sem=csem.at[3],
            device_id={"ctx": to},
            device_id_type=MESH,
        )

    def wait_all(like, i):
        whole = like.at[pl.ds(0, nctx - 1)]
        pltpu.make_async_copy(whole, whole, csem.at[i]).wait()

    for part in range(2):
        rows = slice(part * SLAB, (part + 1) * SLAB)
        for cb in range(ncb):
            cols = slice(cb * COLS, (cb + 1) * COLS)
            d = db[rows, cols] + dot(first[rows], xb[0:128, cols])
            d = (d * rowsb[0:1, cols]).astype(BF16)
            for pair in range(COLS // 128):
                slab_s[(cb * (COLS // 128) + pair) * 2 + part] = d[:, pair * 128 : pair * 128 + 128]

        for quarter in (part, part + 2):

            @pl.when(lax.rem(me, 4) != quarter)
            def _():
                slab_copy((me // 4) * 4 + quarter).start()

            for k in range(1, nctx // 4):
                slab_copy(lax.rem(me // 4 + k, nctx // 4) * 4 + quarter).start()
        if part == 0:
            for k in range(1, nctx):
                total_copy(lax.rem(me + k, nctx)).start()
    slab_r[me] = slab_s[me]
    kt[...] = kb[...].T.astype(BF16)

    for i in range(2):
        score = dot(qb[i * half_t : (i + 1) * half_t, :], kt[...])
        keep = iota((half_t, tokens), 0) + i * half_t >= iota((half_t, tokens), 1)
        mb[i * half_t : (i + 1) * half_t, :] = jnp.where(keep, score, 0.0).astype(BF16)

    def intra(cb, _):
        cols = columns(cb)
        yb[0:half_t, cols] = dot(mb[0:half_t, 0:half_t], xb[0:half_t, cols])
        yb[half_t:tokens, cols] = dot(mb[half_t:tokens, :], xb[:, cols])
        return 0

    lax.fori_loop(0, ncb, intra, 0)

    def back_copy(to):
        rows = pl.ds(pl.multiple_of(lax.rem(me, 2) * SLAB, SLAB), SLAB)
        lanes = pl.ds(pl.multiple_of((me // 2) * 128, 128), 128)
        return pltpu.make_async_remote_copy(
            src_ref=ret_s.at[to],
            dst_ref=inc.at[rows, lanes],
            send_sem=csem.at[4],
            recv_sem=csem.at[5],
            device_id={"ctx": to},
            device_id_type=MESH,
        )

    wait_all(tot, 1)
    lanes = pl.ds(pl.multiple_of((me // 2) * 128, 128), 128)
    everyone = in_three(tot[...].reshape(nctx, 128), iota((nctx, 128), 1) // 32)
    fade[...] = jnp.exp(dot(everyone, oh[:, lanes])).reshape(nctx, 1, 128)

    wait_all(slab_r, 3)

    def scan(i, run):
        for e in range(8):
            ret_s[i * 8 + e] = run.astype(BF16)
            run = fade[i * 8 + e] * run + slab_r[i * 8 + e].astype(F32)
        return run

    lax.fori_loop(0, nctx // 8, scan, jnp.zeros((SLAB, 128), F32))

    for k in range(1, nctx):
        back_copy(lax.rem(me + k, nctx)).start()
    inc[
        pl.ds(pl.multiple_of(lax.rem(me, 2) * SLAB, SLAB), SLAB),
        pl.ds(pl.multiple_of((me // 2) * 128, 128), 128),
    ] = ret_s[me]

    loads[6].wait()

    def gate_block(i, _):
        cols = columns(i // 4)
        at = pl.ds(pl.multiple_of(lax.rem(i, 4) * 128, 128), 128)
        ab[at, cols] = dot(e3[at, :], oh[:, cols]) * silu(gateb[at, cols].astype(F32))
        return 0

    lax.fori_loop(0, ncb * 4, gate_block, 0)
    loads[7].wait()
    loads[8].wait()

    wait_all(ret_s, 5)

    group_n = iota((BLOCK, 128), 1) // 32

    def block_rows(b):
        return pl.ds(pl.multiple_of(b * BLOCK, BLOCK), BLOCK)

    def norm_block(b):
        at = block_rows(b)
        mean = jnp.zeros((BLOCK, 128), F32)
        for cb in range(ncb):
            cols = slice(cb * COLS, (cb + 1) * COLS)
            y = dot(qb[at, :], inc[:, cols]) * rowsb[1:2, cols] + yb[at, cols]
            y = y * ab[at, cols]
            yb[at, cols] = y
            mean = mean + dot((y * y).astype(BF16), oht[cols, :])
        scale = in_three(lax.rsqrt(mean + 1e-05), group_n)
        for cb in range(ncb):
            cols = slice(cb * COLS, (cb + 1) * COLS)
            xb[at, cols] = (yb[at, cols] * dot(scale, oh[:, cols]) * gainb[:, cols]).astype(BF16)

    def project(b, dest, half):
        cols = pl.ds(pl.multiple_of(dest * outs + half * half_o, half_o), half_o)
        return dot(xb[block_rows(b), :], wb[:, cols])

    def towards(side):
        return lax.rem(z + 1 + side * (nhead - 2), nhead)

    def job_copy(src, dst, side, b, first):
        i = (first * nblk + b) * 2 + side
        return pltpu.make_async_remote_copy(
            src_ref=src.at[side, b],
            dst_ref=dst.at[side, b],
            send_sem=js.at[i],
            recv_sem=jr.at[i],
            device_id={"head": towards(side)},
            device_id_type=MESH,
        )

    def relay_block(b, _):
        norm_block(b)

        def one(side, _):
            rel_s[side, b] = project(b, lax.rem(z + 2, nhead), side).astype(BF16)
            job_copy(rel_s, rel_r, side, b, 0).start()
            return 0

        return lax.fori_loop(0, 2, one, 0)

    lax.fori_loop(0, nblk, relay_block, 0)

    def plain(i, _):
        b, side = i // 2, lax.rem(i, 2)
        p_s[side, b] = project(b, towards(side), 1 - side).astype(BF16)
        job_copy(p_s, p_r, side, b, 1).start()
        return 0

    lax.fori_loop(0, 2 * nblk, plain, 0)

    def relayed(i, _):
        b, side = i // 2, lax.rem(i, 2)
        part = project(b, towards(side), side)
        job_copy(rel_s, rel_r, side, b, 0).wait_recv()
        r_s[side, b] = (part + rel_r[side, b].astype(F32)).astype(BF16)
        job_copy(r_s, r_r, side, b, 2).start()
        return 0

    lax.fori_loop(0, 2 * nblk, relayed, 0)

    def mine(i, _):
        b, half = i // 2, lax.rem(i, 2)
        own[half, b] = project(b, z, half)
        return 0

    lax.fori_loop(0, 2 * nblk, mine, 0)

    @pl.when(me < nctx - 1)
    def _():
        for border in borders:
            border.wait_send()

    wait_all(tot, 0)
    wait_all(slab_r, 2)
    wait_all(ret_s, 4)

    def jobs_left(i, _):
        b, side = i // 2, lax.rem(i, 2)
        job_copy(rel_s, rel_r, side, b, 0).wait_send()
        job_copy(p_s, p_r, side, b, 1).wait_send()
        return 0

    lax.fori_loop(0, 2 * nblk, jobs_left, 0)

    def finish(i, _):
        b, half = i // 2, lax.rem(i, 2)
        job_copy(p_s, p_r, 1 - half, b, 1).wait_recv()
        job_copy(r_s, r_r, half, b, 2).wait_send()
        job_copy(r_s, r_r, half, b, 2).wait_recv()
        total = own[half, b] + p_r[1 - half, b].astype(F32) + r_r[half, b].astype(F32)
        out_h[block_rows(b), pl.ds(pl.multiple_of(half * half_o, half_o), half_o)] = total.astype(BF16)
        return 0

    lax.fori_loop(0, 2 * nblk, finish, 0)


def per_device(
    nctx,
    nhead,
    features_in,
    gate_input,
    state_proj,
    step_raw,
    rate_log,
    conv_features,
    conv_states,
    norm_gain,
    out_weight,
):
    tokens, feats = features_in.shape
    heads = rate_log.shape[0]
    outs = out_weight.shape[1] // nhead
    half_o = outs // 2
    any_space = pl.BlockSpec(memory_space=pltpu.HBM)
    vmem = pltpu.VMEM
    dma = pltpu.SemaphoreType.DMA
    job = (2, tokens // BLOCK, BLOCK, half_o)
    scratch = [
        vmem((LEAD + tokens, feats), BF16),
        vmem((tokens, feats), BF16),
        vmem((LEAD + tokens, 2 * STATE), BF16),
        vmem((LEAD, feats), BF16),
        vmem((LEAD, 2 * STATE), BF16),
        vmem((heads, tokens), F32),
        vmem((1, heads), F32),
        vmem((4, feats), F32),
        vmem((4, 2 * STATE), F32),
        vmem((1, feats), F32),
        vmem(out_weight.shape, BF16),
        vmem((tokens, feats), F32),
        vmem((tokens, feats), F32),
        vmem((tokens, feats), BF16),
        vmem((STATE, feats), F32),
        vmem((tokens, STATE), F32),
        vmem((tokens, STATE), BF16),
        vmem((STATE, tokens), BF16),
        vmem((tokens, tokens), BF16),
        vmem((tokens, 128), BF16),
        vmem((tokens, 128), BF16),
        vmem((128, feats), BF16),
        vmem((feats, 128), BF16),
        vmem((16, feats), F32),
        vmem((nctx, 1, 128), F32),
        vmem((nctx, 1, 128), F32),
        vmem((nctx, SLAB, 128), BF16),
        vmem((nctx, SLAB, 128), BF16),
        vmem((nctx, SLAB, 128), BF16),
        vmem((STATE, feats), BF16),
        vmem(job, BF16),
        vmem(job, BF16),
        vmem(job, BF16),
        vmem(job, BF16),
        vmem(job, BF16),
        vmem(job, BF16),
        vmem(job, F32),
        dma((9,)),
        dma((4,)),
        dma((6,)),
        dma((6 * (tokens // BLOCK),)),
        dma((6 * (tokens // BLOCK),)),
    ]
    return pl.pallas_call(
        functools.partial(layer, nctx, nhead),
        out_shape=jax.ShapeDtypeStruct((tokens, outs), BF16),
        in_specs=[any_space] * 9,
        out_specs=pl.BlockSpec(memory_space=pltpu.VMEM),
        scratch_shapes=scratch,
        compiler_params=pltpu.CompilerParams(collective_id=0, has_side_effects=True, vmem_limit_bytes=52 * 1024 * 1024),
        name="ssd_layer",
    )(
        *(
            pltpu.with_memory_space_constraint(a, pltpu.HBM)
            for a in (
                features_in,
                gate_input,
                state_proj,
                step_raw.T,
                rate_log.reshape(1, heads),
                conv_features,
                conv_states,
                norm_gain.reshape(1, feats),
                out_weight,
            )
        )
    )


def solution(mesh):
    placed = (
        P("ctx", "head"),
        P("ctx", "head"),
        P("ctx", None),
        P("ctx", "head"),
        P("head"),
        P(None, "head"),
        P(),
        P("head"),
        P("head", None),
    )
    body = functools.partial(per_device, mesh.shape["ctx"], mesh.shape["head"])
    return jax.shard_map(
        body, mesh=mesh, in_specs=placed, out_specs=P("ctx", "head"), check_vma=False
    )
```

```python
import functools

import jax
import jax.numpy as jnp
from jax import lax
from jax.experimental import pallas as pl
from jax.experimental.pallas import tpu as pltpu
from jax.sharding import PartitionSpec as P

HEAD_DIM = 64
STATE = 128
MESH = pl.DeviceIdType.MESH
F32 = jnp.float32
BF16 = jnp.bfloat16

LEAD = 16
ROWS = 64
BLOCK = 128
COLS = 256
SLAB = 64
GROUPS = 4


def dot(a, b):
    return jnp.dot(a, b, preferred_element_type=F32)


def silu(x):
    half = 0.5 * x
    return half + half * jnp.tanh(half)


def iota(shape, axis):
    return lax.broadcasted_iota(jnp.int32, shape, axis)


def in_three(value, group):
    high = value.astype(BF16).astype(F32)
    rest = value - high
    mid = rest.astype(BF16).astype(F32)
    low = rest - mid
    none = jnp.zeros_like(value)
    parts = jnp.where(group == 0, high, jnp.where(group == 1, mid, jnp.where(group == 2, low, none)))
    return parts.astype(BF16)


def layer(
    nctx,
    nhead,
    feat_h,
    gate_h,
    st_h,
    step_h,
    rate_h,
    taps_h,
    staps_h,
    gain_h,
    w_h,
    out_h,
    featb,
    gateb,
    stb,
    bordf,
    bords,
    stepb,
    rateb,
    tapsb,
    stapsb,
    gainb,
    wb,
    ab,
    yb,
    xb,
    db,
    kb,
    qb,
    kt,
    mb,
    a3,
    e3,
    oh,
    oht,
    rowsb,
    tot,
    fade,
    slab_s,
    slab_r,
    ret_s,
    inc,
    rel_s,
    rel_r,
    p_s,
    p_r,
    r_s,
    r_r,
    own,
    lsem,
    bsem,
    csem,
    js,
    jr,
):
    tokens, feats = gate_h.shape
    half_t = tokens // 2
    outs = out_h.shape[1]
    half_o = outs // 2
    ncb = feats // COLS
    nrow = tokens // ROWS
    nblk = tokens // BLOCK
    me = lax.axis_index("ctx")
    z = lax.axis_index("head")

    loads = [
        (step_h, stepb),
        (rate_h, rateb),
        (st_h, stb.at[pl.ds(LEAD, tokens), :]),
        (staps_h, stapsb),
        (taps_h, tapsb),
        (feat_h, featb.at[pl.ds(LEAD, tokens), :]),
        (gate_h, gateb),
        (gain_h, gainb),
        (w_h, wb),
    ]
    loads = [pltpu.make_async_copy(s, d, lsem.at[i]) for i, (s, d) in enumerate(loads)]
    for load in loads[:6]:
        load.start()

    barrier = pltpu.get_barrier_semaphore()

    def greet(k, _):
        pl.semaphore_signal(
            barrier, inc=1, device_id={"ctx": lax.rem(me + k, nctx)}, device_id_type=MESH
        )
        return 0

    lax.fori_loop(1, nctx, greet, 0)
    for k in (1, nhead - 1):
        pl.semaphore_signal(
            barrier, inc=1, device_id={"head": lax.rem(z + k, nhead)}, device_id_type=MESH
        )

    group = iota((tokens, 128), 1) // 32
    tri = jnp.where(iota((tokens, tokens), 0) >= iota((tokens, tokens), 1), 1.0, 0.0).astype(BF16)
    oh[...] = jnp.where((iota((128, feats), 0) & 31) == iota((128, feats), 1) // HEAD_DIM, 1.0, 0.0).astype(BF16)
    oht[...] = jnp.where(
        (iota((feats, 128), 1) & 31) == iota((feats, 128), 0) // HEAD_DIM, 1.0 / HEAD_DIM, 0.0
    ).astype(BF16)
    featb[0:LEAD, :] = jnp.zeros((LEAD, feats), BF16)
    stb[0:LEAD, :] = jnp.zeros((LEAD, 2 * STATE), BF16)
    loads[0].wait()
    loads[1].wait()
    raw = jnp.concatenate([stepb[...]] * 4, axis=0).T
    step = jnp.maximum(raw, 0.0) + jnp.log(1.0 + jnp.exp(-jnp.abs(raw)))
    rate = jnp.concatenate([rateb[...]] * 4, axis=1)
    decay = in_three(-step * jnp.exp(rate), group)
    thirds = dot(tri, decay)
    cum = (
        thirds
        + pltpu.roll(thirds, 32, 1)
        + pltpu.roll(thirds, 64, 1)
        + pltpu.roll(thirds, 96, 1)
    )
    tot[me] = cum[tokens - 1 : tokens]
    centre = cum[half_t - 1 : half_t]
    total = cum[tokens - 1 : tokens]
    away = cum - centre
    a3[...] = in_three(step * jnp.exp(-away), group)
    e3[...] = in_three(jnp.exp(away), group)
    line = iota((16, 128), 0)
    scales = jnp.where(line == 0, jnp.exp(total - centre), jnp.exp(centre))
    rowsb[...] = dot(in_three(scales, iota((16, 128), 1) // 32), oh[...])

    def conv(x, taps):
        total = x * taps[3:4]
        for back in range(1, 4):
            total = total + pltpu.roll(x, back, 0) * taps[3 - back : 4 - back]
        return silu(total[LEAD:])

    def columns(cb):
        return pl.ds(pl.multiple_of(cb * COLS, COLS), COLS)

    loads[2].wait()
    loads[3].wait()

    def states(r, _):
        at = pl.multiple_of(r * ROWS, ROWS)
        v = conv(stb[pl.ds(at, ROWS + LEAD), :].astype(F32), stapsb[...])
        kb[pl.ds(at, ROWS), :] = v[:, :STATE].astype(BF16).astype(F32)
        qb[pl.ds(at, ROWS), :] = v[:, STATE:].astype(BF16)
        return 0

    lax.fori_loop(0, nrow, states, 0, unroll=True)
    later = iota((tokens, STATE), 0) >= LEAD
    kt[...] = jnp.where(later, kb[...], 0.0).T.astype(BF16)

    loads[4].wait()
    loads[5].wait()
    for load in loads[6:]:
        load.start()

    def feature_block(cb):
        cols = columns(cb)
        ab[:, cols] = dot(a3[...], oh[:, cols])

        def chunk(r, _):
            at = pl.multiple_of(r * ROWS, ROWS)
            x = featb[pl.ds(at, ROWS + LEAD), cols].astype(F32)
            v = conv(x, tapsb[:, cols]) * ab[pl.ds(at, ROWS), cols]
            xb[pl.ds(at, ROWS), cols] = v.astype(BF16)
            return 0

        lax.fori_loop(0, nrow, chunk, 0, unroll=True)

    def state_block(cb):
        cols = columns(cb)
        db[:, cols] = dot(kt[...], xb[:, cols])

    def both(cb, _):
        state_block(cb - 1)
        feature_block(cb)
        return 0

    feature_block(0)
    lax.fori_loop(1, ncb // 2, both, 0)

    pl.semaphore_wait(barrier, nctx + 1)
    after = lax.rem(me + 1, nctx)
    borders = [
        pltpu.make_async_remote_copy(
            src_ref=src.at[pl.ds(tokens, LEAD), :],
            dst_ref=dst,
            send_sem=bsem.at[i],
            recv_sem=bsem.at[2 + i],
            device_id={"ctx": after},
            device_id_type=MESH,
        )
        for i, (src, dst) in enumerate(((featb, bordf), (stb, bords)))
    ]

    @pl.when(me < nctx - 1)
    def _():
        for border in borders:
            border.start()

    @pl.when(me == 0)
    def _():
        bordf[...] = jnp.zeros((LEAD, feats), BF16)
        bords[...] = jnp.zeros((LEAD, 2 * STATE), BF16)

    lax.fori_loop(ncb // 2, ncb, both, 0)
    state_block(ncb - 1)

    @pl.when(me > 0)
    def _():
        for border in borders:
            border.wait_recv()

    v = conv(jnp.concatenate([bords[...], stb[LEAD : 2 * LEAD, :]], axis=0).astype(F32), stapsb[...])
    kb[0:LEAD, :] = v[:, :STATE].astype(BF16).astype(F32)
    qb[0:LEAD, :] = v[:, STATE:].astype(BF16)
    first = jnp.where(iota((128, STATE), 0) < LEAD, kb[0:128, :], 0.0).T.astype(BF16)

    def total_copy(to):
        return pltpu.make_async_remote_copy(
            src_ref=tot.at[me],
            dst_ref=tot.at[me],
            send_sem=csem.at[0],
            recv_sem=csem.at[1],
            device_id={"ctx": to},
            device_id_type=MESH,
        )

    def slab_copy(to):
        return pltpu.make_async_remote_copy(
            src_ref=slab_s.at[to],
            dst_ref=slab_r.at[me],
            send_sem=csem.at[2],
            recv_sem=csem.at[3],
            device_id={"ctx": to},
            device_id_type=MESH,
        )

    def wait_all(like, i):
        whole = like.at[pl.ds(0, nctx - 1)]
        pltpu.make_async_copy(whole, whole, csem.at[i]).wait()

    for g in range(GROUPS):
        for cb in range(g * ncb // GROUPS, (g + 1) * ncb // GROUPS):
            cols = slice(cb * COLS, (cb + 1) * COLS)
            x = jnp.concatenate([bordf[:, cols], featb[LEAD : 2 * LEAD, cols]], axis=0).astype(F32)
            xb[0:LEAD, cols] = (conv(x, tapsb[:, cols]) * ab[0:LEAD, cols]).astype(BF16)
            d = db[:, cols] + dot(first, xb[0:128, cols])
            d = (d * rowsb[0:1, cols]).astype(BF16)
            for pair in range(COLS // 128):
                at = (cb * (COLS // 128) + pair) % 4
                for part in range(2):
                    slab_s[(at * 2 + part) * GROUPS + g] = d[
                        part * SLAB : (part + 1) * SLAB, pair * 128 : pair * 128 + 128
                    ]
        for k in range(1, nctx // GROUPS):
            slab_copy(lax.rem(me // GROUPS + k, nctx // GROUPS) * GROUPS + g).start()

        @pl.when(lax.rem(me, GROUPS) != g)
        def _():
            slab_copy((me // GROUPS) * GROUPS + g).start()

        if g == 1:
            for k in range(1, nctx):
                total_copy(lax.rem(me + k, nctx)).start()
    slab_r[me] = slab_s[me]
    kt[...] = kb[...].T.astype(BF16)

    for i in range(2):
        score = dot(qb[i * half_t : (i + 1) * half_t, :], kt[...])
        keep = iota((half_t, tokens), 0) + i * half_t >= iota((half_t, tokens), 1)
        mb[i * half_t : (i + 1) * half_t, :] = jnp.where(keep, score, 0.0).astype(BF16)

    def intra(cb, _):
        cols = columns(cb)
        yb[0:half_t, cols] = dot(mb[0:half_t, 0:half_t], xb[0:half_t, cols])
        yb[half_t:tokens, cols] = dot(mb[half_t:tokens, :], xb[:, cols])
        return 0

    lax.fori_loop(0, ncb, intra, 0)

    group_me = lax.rem(me, GROUPS)
    my_rows = pl.ds(pl.multiple_of(lax.rem(me // GROUPS, 2) * SLAB, SLAB), SLAB)
    my_lanes = pl.ds(pl.multiple_of((group_me * 4 + me // (2 * GROUPS)) * 128, 128), 128)

    def back_copy(to):
        return pltpu.make_async_remote_copy(
            src_ref=ret_s.at[to],
            dst_ref=inc.at[my_rows, my_lanes],
            send_sem=csem.at[4],
            recv_sem=csem.at[5 + group_me],
            device_id={"ctx": to},
            device_id_type=MESH,
        )

    wait_all(tot, 1)
    everyone = in_three(tot[...].reshape(nctx, 128), iota((nctx, 128), 1) // 32)
    fade[...] = jnp.exp(dot(everyone, oh[:, my_lanes])).reshape(nctx, 1, 128)

    wait_all(slab_r, 3)

    def scan(i, run):
        for e in range(8):
            ret_s[i * 8 + e] = run.astype(BF16)
            run = fade[i * 8 + e] * run + slab_r[i * 8 + e].astype(F32)
        return run

    lax.fori_loop(0, nctx // 8, scan, jnp.zeros((SLAB, 128), F32))

    for k in range(1, nctx):
        back_copy(lax.rem(me + k, nctx)).start()
    inc[my_rows, my_lanes] = ret_s[me]

    loads[6].wait()

    def gate_block(i, _):
        cols = columns(i // 4)
        at = pl.ds(pl.multiple_of(lax.rem(i, 4) * 128, 128), 128)
        gate = dot(e3[at, :], oh[:, cols]) * silu(gateb[at, cols].astype(F32))
        yb[at, cols] = yb[at, cols] * gate
        ab[at, cols] = gate * rowsb[1:2, cols]
        return 0

    lax.fori_loop(0, ncb * 4, gate_block, 0)
    loads[7].wait()
    loads[8].wait()

    def group_here(g):
        for own_one in range(2):

            @pl.when((group_me == g) if own_one else (group_me != g))
            def _():
                some = ret_s.at[pl.ds(0, nctx // GROUPS - own_one)]
                pltpu.make_async_copy(some, some, csem.at[5 + g]).wait()

    group_n = iota((BLOCK, 128), 1) // 32

    def block_rows(b):
        return pl.ds(pl.multiple_of(b * BLOCK, BLOCK), BLOCK)

    def norm(at, blocks):
        mean = jnp.zeros((BLOCK, 128), F32)
        for cb in blocks:
            cols = slice(cb * COLS, (cb + 1) * COLS)
            y = dot(qb[at, :], inc[:, cols]) * ab[at, cols] + yb[at, cols]
            yb[at, cols] = y
            mean = mean + dot((y * y).astype(BF16), oht[cols, :])
        scale = in_three(lax.rsqrt(mean + 1e-05), group_n)
        for cb in blocks:
            cols = slice(cb * COLS, (cb + 1) * COLS)
            xb[at, cols] = (yb[at, cols] * dot(scale, oh[:, cols]) * gainb[:, cols]).astype(BF16)

    def project(b, dest, half):
        cols = pl.ds(pl.multiple_of(dest * outs + half * half_o, half_o), half_o)
        return dot(xb[block_rows(b), :], wb[:, cols])

    def towards(side):
        return lax.rem(z + 1 + side * (nhead - 2), nhead)

    def job_copy(src, dst, side, b, first):
        i = (first * nblk + b) * 2 + side
        return pltpu.make_async_remote_copy(
            src_ref=src.at[side, b],
            dst_ref=dst.at[side, b],
            send_sem=js.at[i],
            recv_sem=jr.at[i],
            device_id={"head": towards(side)},
            device_id_type=MESH,
        )

    for g in range(2):
        group_here(2 * g)
        group_here(2 * g + 1)
        norm(slice(0, BLOCK), range(g * ncb // 2, (g + 1) * ncb // 2))
        feats_g = slice(g * feats // 2, (g + 1) * feats // 2)
        for side in range(2):
            at = lax.rem(z + 2, nhead) * outs + side * half_o
            cols = pl.ds(pl.multiple_of(at, half_o), half_o)
            part = dot(xb[0:BLOCK, feats_g], wb[feats_g, cols])
            if g > 0:
                part = part + own[side, 0]
            if g < 1:
                own[side, 0] = part
            else:
                rel_s[side, 0] = part.astype(BF16)
                job_copy(rel_s, rel_r, side, 0, 0).start()

    def relay_block(b, _):
        norm(block_rows(b), range(ncb))

        def one(side, _):
            rel_s[side, b] = project(b, lax.rem(z + 2, nhead), side).astype(BF16)
            job_copy(rel_s, rel_r, side, b, 0).start()
            return 0

        return lax.fori_loop(0, 2, one, 0)

    lax.fori_loop(1, nblk, relay_block, 0)

    def plain(i, _):
        b, side = i // 2, lax.rem(i, 2)
        p_s[side, b] = project(b, towards(side), 1 - side).astype(BF16)
        job_copy(p_s, p_r, side, b, 1).start()
        return 0

    lax.fori_loop(0, 2 * nblk, plain, 0)

    def relayed(i, _):
        b, side = i // 2, lax.rem(i, 2)
        part = project(b, towards(side), side)
        job_copy(rel_s, rel_r, side, b, 0).wait_recv()
        r_s[side, b] = (part + rel_r[side, b].astype(F32)).astype(BF16)
        job_copy(r_s, r_r, side, b, 2).start()
        return 0

    lax.fori_loop(0, 2 * nblk, relayed, 0)

    def mine(i, _):
        b, half = i // 2, lax.rem(i, 2)
        own[half, b] = project(b, z, half)
        return 0

    lax.fori_loop(0, 2 * nblk, mine, 0)

    @pl.when(me < nctx - 1)
    def _():
        for border in borders:
            border.wait_send()

    wait_all(tot, 0)
    wait_all(slab_r, 2)
    wait_all(ret_s, 4)

    def jobs_left(i, _):
        b, side = i // 2, lax.rem(i, 2)
        job_copy(rel_s, rel_r, side, b, 0).wait_send()
        job_copy(p_s, p_r, side, b, 1).wait_send()
        return 0

    lax.fori_loop(0, 2 * nblk, jobs_left, 0)

    def finish(i, _):
        b, half = i // 2, lax.rem(i, 2)
        job_copy(p_s, p_r, 1 - half, b, 1).wait_recv()
        job_copy(r_s, r_r, half, b, 2).wait_send()
        job_copy(r_s, r_r, half, b, 2).wait_recv()
        total = own[half, b] + p_r[1 - half, b].astype(F32) + r_r[half, b].astype(F32)
        out_h[block_rows(b), pl.ds(pl.multiple_of(half * half_o, half_o), half_o)] = total.astype(BF16)
        return 0

    lax.fori_loop(0, 2 * nblk, finish, 0)


def per_device(
    nctx,
    nhead,
    features_in,
    gate_input,
    state_proj,
    step_raw,
    rate_log,
    conv_features,
    conv_states,
    norm_gain,
    out_weight,
):
    tokens, feats = features_in.shape
    heads = rate_log.shape[0]
    outs = out_weight.shape[1] // nhead
    half_o = outs // 2
    any_space = pl.BlockSpec(memory_space=pltpu.HBM)
    vmem = pltpu.VMEM
    dma = pltpu.SemaphoreType.DMA
    job = (2, tokens // BLOCK, BLOCK, half_o)
    scratch = [
        vmem((LEAD + tokens, feats), BF16),
        vmem((tokens, feats), BF16),
        vmem((LEAD + tokens, 2 * STATE), BF16),
        vmem((LEAD, feats), BF16),
        vmem((LEAD, 2 * STATE), BF16),
        vmem((heads, tokens), F32),
        vmem((1, heads), F32),
        vmem((4, feats), F32),
        vmem((4, 2 * STATE), F32),
        vmem((1, feats), F32),
        vmem(out_weight.shape, BF16),
        vmem((tokens, feats), F32),
        vmem((tokens, feats), F32),
        vmem((tokens, feats), BF16),
        vmem((STATE, feats), F32),
        vmem((tokens, STATE), F32),
        vmem((tokens, STATE), BF16),
        vmem((STATE, tokens), BF16),
        vmem((tokens, tokens), BF16),
        vmem((tokens, 128), BF16),
        vmem((tokens, 128), BF16),
        vmem((128, feats), BF16),
        vmem((feats, 128), BF16),
        vmem((16, feats), F32),
        vmem((nctx, 1, 128), F32),
        vmem((nctx, 1, 128), F32),
        vmem((nctx, SLAB, 128), BF16),
        vmem((nctx, SLAB, 128), BF16),
        vmem((nctx, SLAB, 128), BF16),
        vmem((STATE, feats), BF16),
        vmem(job, BF16),
        vmem(job, BF16),
        vmem(job, BF16),
        vmem(job, BF16),
        vmem(job, BF16),
        vmem(job, BF16),
        vmem(job, F32),
        dma((9,)),
        dma((4,)),
        dma((5 + GROUPS,)),
        dma((6 * (tokens // BLOCK),)),
        dma((6 * (tokens // BLOCK),)),
    ]
    return pl.pallas_call(
        functools.partial(layer, nctx, nhead),
        out_shape=jax.ShapeDtypeStruct((tokens, outs), BF16),
        in_specs=[any_space] * 9,
        out_specs=pl.BlockSpec(memory_space=pltpu.VMEM),
        scratch_shapes=scratch,
        compiler_params=pltpu.CompilerParams(collective_id=0, has_side_effects=True, vmem_limit_bytes=52 * 1024 * 1024),
        name="ssd_layer",
    )(
        *(
            pltpu.with_memory_space_constraint(a, pltpu.HBM)
            for a in (
                features_in,
                gate_input,
                state_proj,
                step_raw.T,
                rate_log.reshape(1, heads),
                conv_features,
                conv_states,
                norm_gain.reshape(1, feats),
                out_weight,
            )
        )
    )


def solution(mesh):
    placed = (
        P("ctx", "head"),
        P("ctx", "head"),
        P("ctx", None),
        P("ctx", "head"),
        P("head"),
        P(None, "head"),
        P(),
        P("head"),
        P("head", None),
    )
    body = functools.partial(per_device, mesh.shape["ctx"], mesh.shape["head"])
    return jax.shard_map(
        body, mesh=mesh, in_specs=placed, out_specs=P("ctx", "head"), check_vma=False
    )
```

```python
import functools

import jax
import jax.numpy as jnp
from jax import lax
from jax.experimental import pallas as pl
from jax.experimental.pallas import tpu as pltpu
from jax.sharding import PartitionSpec as P

HEAD_DIM = 64
STATE = 128
MESH = pl.DeviceIdType.MESH
F32 = jnp.float32
BF16 = jnp.bfloat16

LEAD = 16
ROWS = 128
BLOCK = 128
COLS = 256
SLAB = 64
GROUPS = 4


def dot(a, b):
    return jnp.dot(a, b, preferred_element_type=F32)


def silu(x):
    half = 0.5 * x
    return half + half * jnp.tanh(half)


def iota(shape, axis):
    return lax.broadcasted_iota(jnp.int32, shape, axis)


def in_three(value, group):
    high = value.astype(BF16).astype(F32)
    rest = value - high
    mid = rest.astype(BF16).astype(F32)
    low = rest - mid
    none = jnp.zeros_like(value)
    parts = jnp.where(group == 0, high, jnp.where(group == 1, mid, jnp.where(group == 2, low, none)))
    return parts.astype(BF16)


def layer(
    nctx,
    nhead,
    feat_h,
    gate_h,
    st_h,
    step_h,
    rate_h,
    taps_h,
    staps_h,
    gain_h,
    w_h,
    out_h,
    featb,
    gateb,
    stb,
    bordf,
    bords,
    stepb,
    rateb,
    tapsb,
    stapsb,
    gainb,
    wb,
    ab,
    yb,
    xb,
    db,
    kb,
    qb,
    kt,
    mb,
    a3,
    e3,
    oh,
    oht,
    rowsb,
    tot,
    fade,
    slab_s,
    slab_r,
    ret_s,
    inc,
    rel_s,
    rel_r,
    p_s,
    p_r,
    r_s,
    r_r,
    own,
    lsem,
    bsem,
    csem,
    js,
    jr,
):
    tokens, feats = gate_h.shape
    half_t = tokens // 2
    outs = out_h.shape[1]
    half_o = outs // 2
    ncb = feats // COLS
    nrow = tokens // ROWS
    nblk = tokens // BLOCK
    me = lax.axis_index("ctx")
    z = lax.axis_index("head")

    loads = [
        (step_h, stepb),
        (rate_h, rateb),
        (st_h, stb.at[pl.ds(LEAD, tokens), :]),
        (staps_h, stapsb),
        (taps_h, tapsb),
        (feat_h, featb.at[pl.ds(LEAD, tokens), :]),
        (gate_h, gateb),
        (gain_h, gainb),
        (w_h, wb),
    ]
    loads = [pltpu.make_async_copy(s, d, lsem.at[i]) for i, (s, d) in enumerate(loads)]
    for load in loads[:6]:
        load.start()

    barrier = pltpu.get_barrier_semaphore()

    def greet(k, _):
        pl.semaphore_signal(
            barrier, inc=1, device_id={"ctx": lax.rem(me + k, nctx)}, device_id_type=MESH
        )
        return 0

    lax.fori_loop(1, nctx, greet, 0)
    for k in (1, nhead - 1):
        pl.semaphore_signal(
            barrier, inc=1, device_id={"head": lax.rem(z + k, nhead)}, device_id_type=MESH
        )

    group = iota((tokens, 128), 1) // 32
    tri = jnp.where(iota((tokens, tokens), 0) >= iota((tokens, tokens), 1), 1.0, 0.0).astype(BF16)
    oh[...] = jnp.where((iota((128, feats), 0) & 31) == iota((128, feats), 1) // HEAD_DIM, 1.0, 0.0).astype(BF16)
    oht[...] = jnp.where(
        (iota((feats, 128), 1) & 31) == iota((feats, 128), 0) // HEAD_DIM, 1.0 / HEAD_DIM, 0.0
    ).astype(BF16)
    featb[0:LEAD, :] = jnp.zeros((LEAD, feats), BF16)
    stb[0:LEAD, :] = jnp.zeros((LEAD, 2 * STATE), BF16)
    loads[0].wait()
    loads[1].wait()
    raw = jnp.concatenate([stepb[...]] * 4, axis=0).T
    step = jnp.maximum(raw, 0.0) + jnp.log(1.0 + jnp.exp(-jnp.abs(raw)))
    rate = jnp.concatenate([rateb[...]] * 4, axis=1)
    decay = in_three(-step * jnp.exp(rate), group)
    thirds = dot(tri, decay)
    cum = (
        thirds
        + pltpu.roll(thirds, 32, 1)
        + pltpu.roll(thirds, 64, 1)
        + pltpu.roll(thirds, 96, 1)
    )
    tot[me] = cum[tokens - 1 : tokens]
    centre = cum[half_t - 1 : half_t]
    total = cum[tokens - 1 : tokens]
    away = cum - centre
    a3[...] = in_three(step * jnp.exp(-away), group)
    e3[...] = in_three(jnp.exp(away), group)
    line = iota((16, 128), 0)
    scales = jnp.where(line == 0, jnp.exp(total - centre), jnp.exp(centre))
    rowsb[...] = dot(in_three(scales, iota((16, 128), 1) // 32), oh[...])

    def conv(x, taps):
        total = x * taps[3:4]
        for back in range(1, 4):
            total = total + pltpu.roll(x, back, 0) * taps[3 - back : 4 - back]
        return silu(total[LEAD:])

    def columns(cb):
        return pl.ds(pl.multiple_of(cb * COLS, COLS), COLS)

    loads[2].wait()
    loads[3].wait()

    def states(r, _):
        at = pl.multiple_of(r * ROWS, ROWS)
        v = conv(stb[pl.ds(at, ROWS + LEAD), :].astype(F32), stapsb[...])
        kb[pl.ds(at, ROWS), :] = v[:, :STATE].astype(BF16).astype(F32)
        qb[pl.ds(at, ROWS), :] = v[:, STATE:].astype(BF16)
        return 0

    lax.fori_loop(0, nrow, states, 0, unroll=True)
    later = iota((tokens, STATE), 0) >= LEAD
    kt[...] = jnp.where(later, kb[...], 0.0).T.astype(BF16)

    loads[4].wait()
    loads[5].wait()
    for load in loads[6:]:
        load.start()

    def feature_block(cb):
        cols = columns(cb)
        ab[:, cols] = dot(a3[...], oh[:, cols])

        def chunk(r, _):
            at = pl.multiple_of(r * ROWS, ROWS)
            x = featb[pl.ds(at, ROWS + LEAD), cols].astype(F32)
            v = conv(x, tapsb[:, cols]) * ab[pl.ds(at, ROWS), cols]
            xb[pl.ds(at, ROWS), cols] = v.astype(BF16)
            return 0

        lax.fori_loop(0, nrow, chunk, 0, unroll=True)

    def state_block(cb):
        cols = columns(cb)
        db[:, cols] = dot(kt[...], xb[:, cols])

    def both(cb, _):
        state_block(cb - 1)
        feature_block(cb)
        return 0

    feature_block(0)
    lax.fori_loop(1, ncb // 2, both, 0)

    pl.semaphore_wait(barrier, nctx + 1)
    after = lax.rem(me + 1, nctx)
    borders = [
        pltpu.make_async_remote_copy(
            src_ref=src.at[pl.ds(tokens, LEAD), :],
            dst_ref=dst,
            send_sem=bsem.at[i],
            recv_sem=bsem.at[2 + i],
            device_id={"ctx": after},
            device_id_type=MESH,
        )
        for i, (src, dst) in enumerate(((featb, bordf), (stb, bords)))
    ]

    @pl.when(me < nctx - 1)
    def _():
        for border in borders:
            border.start()

    @pl.when(me == 0)
    def _():
        bordf[...] = jnp.zeros((LEAD, feats), BF16)
        bords[...] = jnp.zeros((LEAD, 2 * STATE), BF16)

    lax.fori_loop(ncb // 2, ncb, both, 0)
    state_block(ncb - 1)

    @pl.when(me > 0)
    def _():
        for border in borders:
            border.wait_recv()

    v = conv(jnp.concatenate([bords[...], stb[LEAD : 2 * LEAD, :]], axis=0).astype(F32), stapsb[...])
    kb[0:LEAD, :] = v[:, :STATE].astype(BF16).astype(F32)
    qb[0:LEAD, :] = v[:, STATE:].astype(BF16)
    first = jnp.where(iota((128, STATE), 0) < LEAD, kb[0:128, :], 0.0).T.astype(BF16)

    def total_copy(to):
        return pltpu.make_async_remote_copy(
            src_ref=tot.at[me],
            dst_ref=tot.at[me],
            send_sem=csem.at[0],
            recv_sem=csem.at[1],
            device_id={"ctx": to},
            device_id_type=MESH,
        )

    def slab_copy(to):
        return pltpu.make_async_remote_copy(
            src_ref=slab_s.at[to],
            dst_ref=slab_r.at[me],
            send_sem=csem.at[2],
            recv_sem=csem.at[3],
            device_id={"ctx": to},
            device_id_type=MESH,
        )

    def wait_all(like, i):
        whole = like.at[pl.ds(0, nctx - 1)]
        pltpu.make_async_copy(whole, whole, csem.at[i]).wait()

    for g in range(GROUPS):
        for cb in range(g * ncb // GROUPS, (g + 1) * ncb // GROUPS):
            cols = slice(cb * COLS, (cb + 1) * COLS)
            x = jnp.concatenate([bordf[:, cols], featb[LEAD : 2 * LEAD, cols]], axis=0).astype(F32)
            xb[0:LEAD, cols] = (conv(x, tapsb[:, cols]) * ab[0:LEAD, cols]).astype(BF16)
            d = db[:, cols] + dot(first, xb[0:128, cols])
            d = (d * rowsb[0:1, cols]).astype(BF16)
            for pair in range(COLS // 128):
                at = (cb * (COLS // 128) + pair) % 4
                for part in range(2):
                    slab_s[(at * 2 + part) * GROUPS + g] = d[
                        part * SLAB : (part + 1) * SLAB, pair * 128 : pair * 128 + 128
                    ]
        for k in range(1, nctx // GROUPS):
            slab_copy(lax.rem(me // GROUPS + k, nctx // GROUPS) * GROUPS + g).start()

        @pl.when(lax.rem(me, GROUPS) != g)
        def _():
            slab_copy((me // GROUPS) * GROUPS + g).start()

        if g == 1:
            for k in range(1, nctx):
                total_copy(lax.rem(me + k, nctx)).start()
    slab_r[me] = slab_s[me]
    kt[...] = kb[...].T.astype(BF16)

    for i in range(2):
        score = dot(qb[i * half_t : (i + 1) * half_t, :], kt[...])
        keep = iota((half_t, tokens), 0) + i * half_t >= iota((half_t, tokens), 1)
        mb[i * half_t : (i + 1) * half_t, :] = jnp.where(keep, score, 0.0).astype(BF16)

    def intra(cb, _):
        cols = columns(cb)
        yb[0:half_t, cols] = dot(mb[0:half_t, 0:half_t], xb[0:half_t, cols])
        yb[half_t:tokens, cols] = dot(mb[half_t:tokens, :], xb[:, cols])
        return 0

    lax.fori_loop(0, ncb, intra, 0)

    group_me = lax.rem(me, GROUPS)
    my_rows = pl.ds(pl.multiple_of(lax.rem(me // GROUPS, 2) * SLAB, SLAB), SLAB)
    my_lanes = pl.ds(pl.multiple_of((group_me * 4 + me // (2 * GROUPS)) * 128, 128), 128)

    def back_copy(to):
        return pltpu.make_async_remote_copy(
            src_ref=ret_s.at[to],
            dst_ref=inc.at[my_rows, my_lanes],
            send_sem=csem.at[4],
            recv_sem=csem.at[5 + group_me],
            device_id={"ctx": to},
            device_id_type=MESH,
        )

    wait_all(tot, 1)
    everyone = in_three(tot[...].reshape(nctx, 128), iota((nctx, 128), 1) // 32)
    fade[...] = jnp.exp(dot(everyone, oh[:, my_lanes])).reshape(nctx, 1, 128)

    wait_all(slab_r, 3)

    def scan(i, run):
        for e in range(8):
            ret_s[i * 8 + e] = run.astype(BF16)
            run = fade[i * 8 + e] * run + slab_r[i * 8 + e].astype(F32)
        return run

    lax.fori_loop(0, nctx // 8, scan, jnp.zeros((SLAB, 128), F32), unroll=True)

    for k in range(1, nctx):
        back_copy(lax.rem(me + k, nctx)).start()
    inc[my_rows, my_lanes] = ret_s[me]

    loads[6].wait()

    def gate_block(i, _):
        cols = columns(i // 4)
        at = pl.ds(pl.multiple_of(lax.rem(i, 4) * 128, 128), 128)
        gate = dot(e3[at, :], oh[:, cols]) * silu(gateb[at, cols].astype(F32))
        yb[at, cols] = yb[at, cols] * gate
        ab[at, cols] = gate * rowsb[1:2, cols]
        return 0

    lax.fori_loop(0, ncb * 4, gate_block, 0)
    loads[7].wait()
    loads[8].wait()

    def group_here(g):
        for own_one in range(2):

            @pl.when((group_me == g) if own_one else (group_me != g))
            def _():
                some = ret_s.at[pl.ds(0, nctx // GROUPS - own_one)]
                pltpu.make_async_copy(some, some, csem.at[5 + g]).wait()

    group_n = iota((BLOCK, 128), 1) // 32

    def block_rows(b):
        return pl.ds(pl.multiple_of(b * BLOCK, BLOCK), BLOCK)

    def norm(at, blocks):
        mean = jnp.zeros((BLOCK, 128), F32)
        for cb in blocks:
            cols = slice(cb * COLS, (cb + 1) * COLS)
            y = dot(qb[at, :], inc[:, cols]) * ab[at, cols] + yb[at, cols]
            yb[at, cols] = y
            mean = mean + dot((y * y).astype(BF16), oht[cols, :])
        scale = in_three(lax.rsqrt(mean + 1e-05), group_n)
        for cb in blocks:
            cols = slice(cb * COLS, (cb + 1) * COLS)
            xb[at, cols] = (yb[at, cols] * dot(scale, oh[:, cols]) * gainb[:, cols]).astype(BF16)

    def project(b, dest, half):
        cols = pl.ds(pl.multiple_of(dest * outs + half * half_o, half_o), half_o)
        return dot(xb[block_rows(b), :], wb[:, cols])

    def towards(side):
        return lax.rem(z + 1 + side * (nhead - 2), nhead)

    def job_copy(src, dst, side, b, first):
        i = (first * nblk + b) * 2 + side
        return pltpu.make_async_remote_copy(
            src_ref=src.at[side, b],
            dst_ref=dst.at[side, b],
            send_sem=js.at[i],
            recv_sem=jr.at[i],
            device_id={"head": towards(side)},
            device_id_type=MESH,
        )

    for g in range(2):
        group_here(2 * g)
        group_here(2 * g + 1)
        norm(slice(0, BLOCK), range(g * ncb // 2, (g + 1) * ncb // 2))
        feats_g = slice(g * feats // 2, (g + 1) * feats // 2)
        for side in range(2):
            at = lax.rem(z + 2, nhead) * outs + side * half_o
            cols = pl.ds(pl.multiple_of(at, half_o), half_o)
            part = dot(xb[0:BLOCK, feats_g], wb[feats_g, cols])
            if g > 0:
                part = part + own[side, 0]
            if g < 1:
                own[side, 0] = part
            else:
                rel_s[side, 0] = part.astype(BF16)
                job_copy(rel_s, rel_r, side, 0, 0).start()

    def relay_block(b, _):
        norm(block_rows(b), range(ncb))

        def one(side, _):
            rel_s[side, b] = project(b, lax.rem(z + 2, nhead), side).astype(BF16)
            job_copy(rel_s, rel_r, side, b, 0).start()
            return 0

        return lax.fori_loop(0, 2, one, 0)

    lax.fori_loop(1, nblk, relay_block, 0)

    def plain(i, _):
        b, side = i // 2, lax.rem(i, 2)
        p_s[side, b] = project(b, towards(side), 1 - side).astype(BF16)
        job_copy(p_s, p_r, side, b, 1).start()
        return 0

    lax.fori_loop(0, 2 * nblk, plain, 0)

    def relayed(i, _):
        b, side = i // 2, lax.rem(i, 2)
        part = project(b, towards(side), side)
        job_copy(rel_s, rel_r, side, b, 0).wait_recv()
        r_s[side, b] = (part + rel_r[side, b].astype(F32)).astype(BF16)
        job_copy(r_s, r_r, side, b, 2).start()
        return 0

    lax.fori_loop(0, 2 * nblk, relayed, 0)

    def mine(i, _):
        b, half = i // 2, lax.rem(i, 2)
        own[half, b] = project(b, z, half)
        return 0

    lax.fori_loop(0, 2 * nblk, mine, 0)

    @pl.when(me < nctx - 1)
    def _():
        for border in borders:
            border.wait_send()

    wait_all(tot, 0)
    wait_all(slab_r, 2)
    wait_all(ret_s, 4)

    def jobs_left(i, _):
        b, side = i // 2, lax.rem(i, 2)
        job_copy(rel_s, rel_r, side, b, 0).wait_send()
        job_copy(p_s, p_r, side, b, 1).wait_send()
        return 0

    lax.fori_loop(0, 2 * nblk, jobs_left, 0)

    def finish(i, _):
        b, half = i // 2, lax.rem(i, 2)
        job_copy(p_s, p_r, 1 - half, b, 1).wait_recv()
        job_copy(r_s, r_r, half, b, 2).wait_send()
        job_copy(r_s, r_r, half, b, 2).wait_recv()
        total = own[half, b] + p_r[1 - half, b].astype(F32) + r_r[half, b].astype(F32)
        out_h[block_rows(b), pl.ds(pl.multiple_of(half * half_o, half_o), half_o)] = total.astype(BF16)
        return 0

    lax.fori_loop(0, 2 * nblk, finish, 0)


def per_device(
    nctx,
    nhead,
    features_in,
    gate_input,
    state_proj,
    step_raw,
    rate_log,
    conv_features,
    conv_states,
    norm_gain,
    out_weight,
):
    tokens, feats = features_in.shape
    heads = rate_log.shape[0]
    outs = out_weight.shape[1] // nhead
    half_o = outs // 2
    any_space = pl.BlockSpec(memory_space=pltpu.HBM)
    vmem = pltpu.VMEM
    dma = pltpu.SemaphoreType.DMA
    job = (2, tokens // BLOCK, BLOCK, half_o)
    scratch = [
        vmem((LEAD + tokens, feats), BF16),
        vmem((tokens, feats), BF16),
        vmem((LEAD + tokens, 2 * STATE), BF16),
        vmem((LEAD, feats), BF16),
        vmem((LEAD, 2 * STATE), BF16),
        vmem((heads, tokens), F32),
        vmem((1, heads), F32),
        vmem((4, feats), F32),
        vmem((4, 2 * STATE), F32),
        vmem((1, feats), F32),
        vmem(out_weight.shape, BF16),
        vmem((tokens, feats), F32),
        vmem((tokens, feats), F32),
        vmem((tokens, feats), BF16),
        vmem((STATE, feats), F32),
        vmem((tokens, STATE), F32),
        vmem((tokens, STATE), BF16),
        vmem((STATE, tokens), BF16),
        vmem((tokens, tokens), BF16),
        vmem((tokens, 128), BF16),
        vmem((tokens, 128), BF16),
        vmem((128, feats), BF16),
        vmem((feats, 128), BF16),
        vmem((16, feats), F32),
        vmem((nctx, 1, 128), F32),
        vmem((nctx, 1, 128), F32),
        vmem((nctx, SLAB, 128), BF16),
        vmem((nctx, SLAB, 128), BF16),
        vmem((nctx, SLAB, 128), BF16),
        vmem((STATE, feats), BF16),
        vmem(job, BF16),
        vmem(job, BF16),
        vmem(job, BF16),
        vmem(job, BF16),
        vmem(job, BF16),
        vmem(job, BF16),
        vmem(job, F32),
        dma((9,)),
        dma((4,)),
        dma((5 + GROUPS,)),
        dma((6 * (tokens // BLOCK),)),
        dma((6 * (tokens // BLOCK),)),
    ]
    return pl.pallas_call(
        functools.partial(layer, nctx, nhead),
        out_shape=jax.ShapeDtypeStruct((tokens, outs), BF16),
        in_specs=[any_space] * 9,
        out_specs=pl.BlockSpec(memory_space=pltpu.VMEM),
        scratch_shapes=scratch,
        compiler_params=pltpu.CompilerParams(collective_id=0, has_side_effects=True, vmem_limit_bytes=52 * 1024 * 1024),
        name="ssd_layer",
    )(
        *(
            pltpu.with_memory_space_constraint(a, pltpu.HBM)
            for a in (
                features_in,
                gate_input,
                state_proj,
                step_raw.T,
                rate_log.reshape(1, heads),
                conv_features,
                conv_states,
                norm_gain.reshape(1, feats),
                out_weight,
            )
        )
    )


def solution(mesh):
    placed = (
        P("ctx", "head"),
        P("ctx", "head"),
        P("ctx", None),
        P("ctx", "head"),
        P("head"),
        P(None, "head"),
        P(),
        P("head"),
        P("head", None),
    )
    body = functools.partial(per_device, mesh.shape["ctx"], mesh.shape["head"])
    return jax.shard_map(
        body, mesh=mesh, in_specs=placed, out_specs=P("ctx", "head"), check_vma=False
    )
```
